256 devices in a mesh: dp: 8 (over z_hi, core), expert: 32 (over z_lo, x, y).
Axes of the slice: x: 4, y: 4, z: 8 (z_hi: 4, z_lo: 2; z = z_hi * 2 + z_lo), core: 2. Of those that a mesh axis runs over, the one named last changes fastest.
Arguments:
- tokens: bfloat16 [32768, 2048], P(('dp', 'expert')), may hold values from -6 to 6
- grad_out: bfloat16 [32768, 768], P(('dp', 'expert')), may hold values from -6 to 6
- expert_ids: int32 [32768, 8], P(('dp', 'expert')), may hold values from 0 to 31, all different within a row; in each aligned block of 128 rows (0 to 127, 128 to 255, ...) at most 36 rows name the same one
- gate_probs: float32 [32768, 8], P(('dp', 'expert')), may hold values from 0.03 to 0.3
- owner: int32 [32], replicated, may hold values from 0 to 31, each once
- partner: int32 [32], replicated, may hold values from 0 to 31, as said below
- weight: bfloat16 [32, 2048, 1536], P('expert', 'dp'), may hold values from -0.125 to 0.125
- first_moment: bfloat16 [32, 2048, 1536], P('expert', 'dp'), may hold values from -5.40625 to 5.40625
- second_moment: bfloat16 [32, 2048, 1536], P('expert', 'dp'), may hold values from 4.09375 to 40.75
Outputs:
- adam_step: float32 [32, 2048, 1536], P('expert', 'dp')
The draws below stay inside these ranges and needn't reach their ends.
Inputs may be any that keep to these rules, and one draw needn't show every extreme that they name: `expert_ids`: among the choices of one device's 128 tokens (aligned blocks of tokens) no expert is named more than 36 times, a bound that some block reaches; a token names 8 different experts. `owner`: each slot appears once. partner[i] is i or (i + 16) % 32, partner[partner[i]] = i, and at least one pair differs.
All inputs are finite; a program needn't handle non-finite values.
Results may differ from the reference program's by a relative error of at most 0.007.
Values may be sent and summed in bfloat16 or wider, within the bound.
A program may use at most 128 MiB of HBM per device.

```python
import math
import jax
import jax.numpy as jnp
import numpy as np
from jax import lax

D = 2048
HID = 768
TOP = 8
TOK_DEV = 128
EXPERTS = 32
CAP = 36
GROUP = 4096
TOKENS = 32768
ROWS = 8192
N_DP = 8
N_EXPERT = 32


def draw_partner(key, part):
    half_way = EXPERTS // 2
    swap_flags = jax.random.randint(jax.random.fold_in(key, 11), (half_way,), 0, 2)
    forced_pair = jax.random.randint(jax.random.fold_in(key, 12), (), 0, half_way)
    swap_flags = jnp.where(jnp.arange(half_way) == forced_pair, 1, swap_flags)
    labels = jnp.arange(EXPERTS, dtype=jnp.int32)
    chosen = swap_flags[labels % half_way]
    shifted = (labels + half_way) % EXPERTS
    return jnp.where(chosen == 1, shifted, labels).astype(jnp.int32)


def level_of(own_key, shape, shards, low, high):
    gain, own = 1.0, jax.random.fold_in(own_key, 6)
    for axis_at, parts in shards:
        steps = jnp.exp(jax.random.uniform(jax.random.fold_in(own, axis_at), (parts,), jnp.float32, low / len(shards), high / len(shards)))
        gain = gain * jnp.repeat(steps, shape[axis_at] // parts).reshape([-1 if axis == axis_at else 1 for axis in range(len(shape))])
    return gain


def routed_block(key, own, number, rows, count, top, bound, skew):
    order = jax.random.permutation(key, count)
    crowded, common = portions_of(count, rows * top, bound, skew, True), portions_of(count, rows * top, bound, skew, False)
    places = jnp.arange(count)

    def named(sizes, turn):
        used = int((sizes > 0).sum())
        fixed = max(1, used // 4)
        passed = fixed + (places - fixed + turn * (used - fixed)) % max(1, count - fixed)
        return jnp.zeros((count,), jnp.int32).at[order[jnp.where(places < fixed, places, passed)]].set(jnp.asarray(sizes, jnp.int32))

    sizes = jnp.where(number % 4 == 0, named(crowded, number // 4), named(common, number - number // 4 - 1))
    mixed = jax.random.permutation(jax.random.fold_in(own, 3), count)
    source_of, receiver = mixed[0:count // 2 * 2:2], mixed[1:count // 2 * 2:2]
    room = jnp.minimum(sizes[source_of] - 1, bound - sizes[receiver]) // 2
    room = jnp.where((source_of == order[0]) | (receiver == order[0]) | (sizes[receiver] == 0), 0, jnp.maximum(room, 0))
    passed = jax.random.randint(jax.random.fold_in(own, 4), (count // 2,), 0, 1 << 20) % (room + 1)
    sizes = sizes.at[source_of].add(-passed).at[receiver].add(passed)
    items = jnp.searchsorted(jnp.cumsum(sizes), jnp.arange(rows * top), side="right").astype(jnp.int32)
    table = items.reshape(top, rows).T
    table = table[jax.random.permutation(jax.random.fold_in(own, 1), rows)]
    turn = jax.random.randint(jax.random.fold_in(own, 2), (rows, 1), 0, top)
    return jnp.take_along_axis(table, (jnp.arange(top)[None, :] + turn) % top, axis=1)


def portions_of(number_of, total, bound, lean, full):
    portions = [(1 << 20) // math.isqrt(rank ** lean) + 1 for rank in range(1, number_of + 1)]
    largest = bound if full else min(bound, max(-(-total // number_of), total * portions[0] // sum(portions)))
    least = 1 if total - largest >= number_of - 1 else 0
    given, spare = [largest] + [least] * (number_of - 1), total - largest - least * (number_of - 1)
    while spare > 0:
        free = [i for i in range(1, number_of) if given[i] < largest] or [i for i in range(1, number_of) if given[i] < bound]
        pool, budget = sum([portions[i] for i in free]), spare
        for i in free:
            extra = min(bound - given[i], max(1, budget * portions[i] // pool), spare)
            given[i] = given[i] + extra
            spare = spare - extra
    return np.array(given)


def scatter_about(stream_key, shape, spread, most, pieces=(), held_as=jnp.bfloat16):
    array = jax.random.normal(stream_key, shape, jnp.float32) * spread
    if len(pieces) > 0:
        array = level_of(stream_key, shape, pieces, -0.22, 0.18) * array
    return jnp.clip(array, min=-most, max=most).astype(held_as)


def setup_inputs(seed: int = 0) -> dict:
    key_list = jax.random.split(jax.random.key(seed), 10)
    tokens = scatter_about(key_list[0], (TOKENS, D), 1.0, 6.0, ((0, 256),))
    grad_out = scatter_about(key_list[1], (TOKENS, HID), 1.0, 6.0, ((0, 256),))
    expert_ids_keys = jax.random.split(jax.random.fold_in(key_list[2], 1), TOKENS // TOK_DEV)
    expert_ids_turns = jax.random.permutation(jax.random.fold_in(key_list[2], 3), TOKENS // TOK_DEV)
    expert_ids = jax.vmap(lambda own, number: routed_block(jax.random.fold_in(key_list[2], 2), own, number, TOK_DEV, EXPERTS, TOP, CAP, 2))(expert_ids_keys, expert_ids_turns).reshape((TOKENS, TOP))
    gate_probs = jnp.clip(jnp.exp(math.log(0.3) - 2.3025852 * jax.random.uniform(key_list[3], (TOKENS, TOP), jnp.float32) ** level_of(key_list[3], (TOKENS, TOP), ((0, 256),), -0.2, 0.2)), 0.03, 0.3)
    owner = jax.random.permutation(key_list[4], EXPERTS).astype(jnp.int32)
    partner = draw_partner(jax.random.fold_in(key_list[9], 71), 0)
    weight = scatter_about(key_list[6], (EXPERTS, D, 2 * HID), D ** -0.5, 0.125, ((0, 32), (1, 8)))
    first_moment = scatter_about(key_list[7], (EXPERTS, D, 2 * HID), (0.01 * ROWS ** 0.5), 5.40625, ((0, 32), (1, 8)))
    second_moment = jnp.clip(jnp.exp(math.log(40.75) - 2.2979944 * jax.random.uniform(key_list[8], (EXPERTS, D, 2 * HID), jnp.float32) ** level_of(key_list[8], (EXPERTS, D, 2 * HID), ((0, 32), (1, 8)), -0.2, 0.2)), 4.09375, 40.75).astype(jnp.bfloat16)
    return {"tokens": tokens, "grad_out": grad_out, "expert_ids": expert_ids, "gate_probs": gate_probs, "owner": owner, "partner": partner, "weight": weight, "first_moment": first_moment, "second_moment": second_moment}


BETA_ONE = 0.9
BETA_TWO = 0.95
EPSILON = 1e-08

def expert_partial(rows_in, rows_grad, weight_slot):
    width_hidden = weight_slot.shape[1] // 2
    pre_act = jnp.dot(rows_in, weight_slot, preferred_element_type=jnp.float32)
    back = rows_grad.astype(jnp.float32)
    gate_part = pre_act[:, :width_hidden]
    up_part = pre_act[:, width_hidden:]
    sigma = jax.nn.sigmoid(gate_part)
    silu_value = gate_part * sigma
    slope = sigma * (1.0 + gate_part * (1.0 - sigma))
    delta = jnp.concatenate([back * up_part * slope, back * silu_value], axis=1).astype(jnp.bfloat16)
    first_part = jnp.dot(rows_in.T, delta, preferred_element_type=jnp.float32)
    return first_part.astype(jnp.bfloat16)

def reference(tokens, grad_out, expert_ids, gate_probs, owner, partner, weight, first_moment, second_moment):
    per_source = TOK_DEV * TOP
    slots_total = N_EXPERT * CAP
    labels = jnp.arange(EXPERTS, dtype=jnp.int32)

    def one_group(total, group):
        start_row = (group * GROUP).astype(jnp.int32)
        x_group = lax.dynamic_slice_in_dim(tokens, start_row, GROUP, 0)
        dy_group = lax.dynamic_slice_in_dim(grad_out, start_row, GROUP, 0)
        id_group = lax.dynamic_slice_in_dim(expert_ids, start_row, GROUP, 0).reshape(-1)
        prob_group = lax.dynamic_slice_in_dim(gate_probs, start_row, GROUP, 0)
        onehot = (id_group[:, None] == labels[None, :]).astype(jnp.int32)
        blocks = onehot.reshape(N_EXPERT, per_source, EXPERTS)
        earlier = (jnp.cumsum(blocks, axis=1) - blocks).reshape(-1, EXPERTS)
        ranks = lax.optimization_barrier(jnp.sum(earlier * onehot, axis=1))
        target = lax.optimization_barrier(jnp.sum(onehot * owner[None, :], axis=1))
        sources = jnp.arange(GROUP * TOP, dtype=jnp.int32) // per_source
        position = target * slots_total + sources * CAP + ranks
        x_rows = jnp.repeat(x_group, TOP, axis=0)
        g_rows = (prob_group[:, :, None] * dy_group[:, None, :].astype(jnp.float32)).astype(jnp.bfloat16).reshape(-1, HID)
        x_buf = jnp.zeros((EXPERTS * slots_total, D), jnp.bfloat16).at[position].set(x_rows).reshape(EXPERTS, slots_total, D)
        g_buf = jnp.zeros((EXPERTS * slots_total, HID), jnp.bfloat16).at[position].set(g_rows).reshape(EXPERTS, slots_total, HID)
        partial_value = lax.map(lambda items: expert_partial(items[0], items[1], items[2]), (x_buf, g_buf, weight))
        return (total + partial_value.astype(jnp.float32), None)
    start_total = jnp.zeros(weight.shape, jnp.float32)
    grads, _ = lax.scan(one_group, start_total, jnp.arange(N_DP, dtype=jnp.int32))
    first_new = BETA_ONE * first_moment.astype(jnp.float32) + (1.0 - BETA_ONE) * grads
    second_new = BETA_TWO * second_moment.astype(jnp.float32) + (1.0 - BETA_TWO) * grads * grads
    step = first_new / (jnp.sqrt(second_new) + EPSILON)
    return step[partner]
```

```python
import jax
import jax.numpy as jnp
from jax import lax
from jax.sharding import PartitionSpec as P

BETA_ONE = 0.9
BETA_TWO = 0.95
EPSILON = 1e-08


def from_partner(value, axis, bit):
    mask = 2**bit
    pairs = [(source, source ^ mask) for source in range(lax.axis_size(axis))]
    return lax.ppermute(value, axis, pairs)


def routed_rows(tokens, grad_out, slots, gate_probs, peers, capacity):
    count, width = tokens.shape
    labels = jnp.arange(peers, dtype=jnp.int32)
    hit = slots[None, :, :] == labels[:, None, None]
    chosen = jnp.any(hit, axis=2)
    gates = jnp.sum(jnp.where(hit, gate_probs[None], 0.0), axis=2)
    before = jnp.arange(count)[:, None] < jnp.arange(count)[None, :]
    ranks = jnp.dot(
        chosen.astype(jnp.bfloat16), before.astype(jnp.bfloat16), preferred_element_type=jnp.float32
    ).astype(jnp.int32)
    ranks = jnp.where(chosen, ranks, -1)
    picks = ranks[:, None, :] == jnp.arange(capacity, dtype=jnp.int32)[None, :, None]
    row_gate = jnp.sum(jnp.where(picks, gates[:, None, :], 0.0), axis=2)
    picks = picks.astype(jnp.bfloat16)
    x_buf = jnp.einsum("brt,td->brd", picks, tokens, preferred_element_type=jnp.float32)
    g_buf = jnp.einsum("brt,td->brd", picks, grad_out, preferred_element_type=jnp.float32)
    return x_buf.astype(jnp.bfloat16), (g_buf * row_gate[:, :, None]).astype(jnp.bfloat16)


def body(
    tokens, grad_out, expert_ids, gate_probs, owner, partner, weight, first_moment, second_moment
):
    peers = lax.axis_size("expert")
    my_index = lax.axis_index("expert")
    swap_bit = peers.bit_length() - 2
    top_k = expert_ids.shape[1]
    expert_count = owner.shape[0]
    capacity = tokens.shape[0] * top_k * 9 // (8 * expert_count)
    width_hidden = weight.shape[2] // 2
    width = tokens.shape[1]
    labels = jnp.arange(expert_count, dtype=jnp.int32)
    moved = jnp.sum(jnp.where(labels == my_index, partner, 0)) != my_index
    slots = jnp.sum(jnp.where(expert_ids[:, :, None] == labels, owner, 0), axis=2)
    x_buf, g_buf = routed_rows(tokens, grad_out, slots, gate_probs, peers, capacity)
    x_recv, g_recv = (
        lax.all_to_all(x_buf, "expert", split_axis=0, concat_axis=0, tiled=True),
        lax.all_to_all(g_buf, "expert", split_axis=0, concat_axis=0, tiled=True),
    )
    rows_in = x_recv.reshape(-1, width)
    rows_grad = g_recv.reshape(-1, g_recv.shape[2])
    pre_act = jnp.dot(
        rows_in,
        lax.all_gather(weight, "dp", axis=1, tiled=True)[0],
        preferred_element_type=jnp.float32,
    )
    back = rows_grad.astype(jnp.float32)
    gate_part = pre_act[:, :width_hidden]
    up_part = pre_act[:, width_hidden:]
    sigma = jax.nn.sigmoid(gate_part)
    silu_value = gate_part * sigma
    slope = sigma * (1.0 + gate_part * (1.0 - sigma))
    delta = jnp.concatenate([back * up_part * slope, back * silu_value], axis=1).astype(
        jnp.bfloat16
    )
    contract = (((0,), (0,)), ((), ()))
    grads = lax.psum_scatter(
        lax.dot_general(rows_in, delta, contract, preferred_element_type=jnp.float32).astype(
            jnp.bfloat16
        ),
        "dp",
        scatter_dimension=0,
        tiled=True,
    ).astype(jnp.float32)
    first_new = BETA_ONE * first_moment[0].astype(jnp.float32) + (1.0 - BETA_ONE) * grads
    second_new = BETA_TWO * second_moment[0].astype(jnp.float32) + (1.0 - BETA_TWO) * grads * grads
    step = first_new / (jnp.sqrt(second_new) + EPSILON)
    arrived = from_partner(step.astype(jnp.bfloat16), "expert", swap_bit)
    return jnp.where(moved, arrived.astype(jnp.float32), step)[None]


def solution(mesh):
    in_specs = (
        P(("dp", "expert"), None),
        P(("dp", "expert"), None),
        P(("dp", "expert"), None),
        P(("dp", "expert"), None),
        P(),
        P(),
        P("expert", "dp", None),
        P("expert", "dp", None),
        P("expert", "dp", None),
    )
    out_specs = P("expert", "dp", None)
    return jax.shard_map(body, mesh=mesh, in_specs=in_specs, out_specs=out_specs, check_vma=False)
```

```python
import jax
import jax.numpy as jnp
from jax import lax
from jax.sharding import PartitionSpec as P

BETA_ONE = 0.9
BETA_TWO = 0.95
EPSILON = 1e-08


def from_partner(value, axis, bit):
    mask = 2**bit
    pairs = [(source, source ^ mask) for source in range(lax.axis_size(axis))]
    return lax.ppermute(value, axis, pairs)


def plane_gates(slots, gate_probs, peers):
    labels = jnp.arange(peers, dtype=jnp.int32)
    hit = slots[None, :, :] == labels[:, None, None]
    return jnp.sum(jnp.where(hit, gate_probs[None], 0.0), axis=2)


def routed_rows(rows, gates, width, capacity):
    peers, count = gates.shape
    chosen = gates > 0.0
    before = jnp.arange(count)[:, None] < jnp.arange(count)[None, :]
    ranks = jnp.dot(
        chosen.astype(jnp.bfloat16), before.astype(jnp.bfloat16), preferred_element_type=jnp.float32
    ).astype(jnp.int32)
    ranks = jnp.where(chosen, ranks, -1)
    picks = ranks[:, None, :] == jnp.arange(capacity, dtype=jnp.int32)[None, :, None]
    row_gate = jnp.sum(jnp.where(picks, gates[:, None, :], 0.0), axis=2)
    picks = picks.astype(jnp.bfloat16).reshape(peers * capacity, count)
    buf = jnp.dot(picks, rows, preferred_element_type=jnp.float32)
    is_grad = jnp.arange(rows.shape[1]) >= width
    scale = jnp.where(is_grad[None, :], row_gate.reshape(-1)[:, None], 1.0)
    return (buf * scale).astype(jnp.bfloat16).reshape(peers, capacity, -1)


def body(
    tokens, grad_out, expert_ids, gate_probs, owner, partner, weight, first_moment, second_moment
):
    peers = lax.axis_size("expert")
    my_index = lax.axis_index("expert")
    swap_bit = peers.bit_length() - 2
    top_k = expert_ids.shape[1]
    expert_count = owner.shape[0]
    capacity = tokens.shape[0] * top_k * 9 // (8 * expert_count)
    width_hidden = weight.shape[2] // 2
    width = tokens.shape[1]
    labels = jnp.arange(expert_count, dtype=jnp.int32)
    moved = jnp.sum(jnp.where(labels == my_index, partner, 0)) != my_index
    slots = jnp.sum(jnp.where(expert_ids[:, :, None] == labels, owner, 0), axis=2)
    half = peers // 2
    upper = my_index >= half
    gates = plane_gates(slots, gate_probs, peers)
    low_gates, high_gates = gates[:half], gates[half:]
    packed = jnp.concatenate([tokens, grad_out], axis=1)
    other_rows = from_partner(packed, "expert", swap_bit)
    other_gates = from_partner(jnp.where(upper, low_gates, high_gates), "expert", swap_bit)
    other_rows, weight = lax.optimization_barrier((other_rows, weight))
    buf = routed_rows(
        jnp.concatenate([packed, other_rows], axis=0),
        jnp.concatenate([jnp.where(upper, high_gates, low_gates), other_gates], axis=1),
        width,
        2 * capacity,
    )
    planes = [list(range(half)), list(range(half, peers))]
    recv = lax.all_to_all(
        buf, "expert", split_axis=0, concat_axis=0, tiled=True, axis_index_groups=planes
    ).reshape(half * 2 * capacity, -1)
    rows_in = recv[:, :width]
    rows_grad = recv[:, width:]
    pre_act = jnp.dot(
        rows_in,
        lax.all_gather(weight, "dp", axis=1, tiled=True)[0],
        preferred_element_type=jnp.float32,
    )
    back = rows_grad.astype(jnp.float32)
    gate_part = pre_act[:, :width_hidden]
    up_part = pre_act[:, width_hidden:]
    sigma = jax.nn.sigmoid(gate_part)
    silu_value = gate_part * sigma
    slope = sigma * (1.0 + gate_part * (1.0 - sigma))
    delta = jnp.concatenate([back * up_part * slope, back * silu_value], axis=1).astype(
        jnp.bfloat16
    )
    contract = (((0,), (0,)), ((), ()))
    grads = lax.psum_scatter(
        lax.dot_general(rows_in, delta, contract, preferred_element_type=jnp.float32).astype(
            jnp.bfloat16
        ),
        "dp",
        scatter_dimension=0,
        tiled=True,
    ).astype(jnp.float32)
    first_new = BETA_ONE * first_moment[0].astype(jnp.float32) + (1.0 - BETA_ONE) * grads
    second_new = BETA_TWO * second_moment[0].astype(jnp.float32) + (1.0 - BETA_TWO) * grads * grads
    step = first_new / (jnp.sqrt(second_new) + EPSILON)
    arrived = from_partner(step.astype(jnp.bfloat16), "expert", swap_bit)
    return jnp.where(moved, arrived.astype(jnp.float32), step)[None]


def solution(mesh):
    in_specs = (
        P(("dp", "expert"), None),
        P(("dp", "expert"), None),
        P(("dp", "expert"), None),
        P(("dp", "expert"), None),
        P(),
        P(),
        P("expert", "dp", None),
        P("expert", "dp", None),
        P("expert", "dp", None),
    )
    out_specs = P("expert", "dp", None)
    return jax.shard_map(body, mesh=mesh, in_specs=in_specs, out_specs=out_specs, check_vma=False)
```

```python
import jax
import jax.numpy as jnp
from jax import lax
from jax.sharding import PartitionSpec as P

BETA_ONE = 0.9
BETA_TWO = 0.95
EPSILON = 1e-08


def from_partner(value, axis, bit):
    mask = 2**bit
    pairs = [(source, source ^ mask) for source in range(lax.axis_size(axis))]
    return lax.ppermute(value, axis, pairs)


def plane_gates(slots, gate_probs, peers):
    labels = jnp.arange(peers, dtype=jnp.int32)
    hit = slots[None, :, :] == labels[:, None, None]
    return jnp.sum(jnp.where(hit, gate_probs[None], 0.0), axis=2)


def routed_rows(rows, gates, width, capacity):
    peers, count = gates.shape
    chosen = gates > 0.0
    before = jnp.arange(count)[:, None] < jnp.arange(count)[None, :]
    ranks = jnp.dot(
        chosen.astype(jnp.bfloat16), before.astype(jnp.bfloat16), preferred_element_type=jnp.float32
    ).astype(jnp.int32)
    ranks = jnp.where(chosen, ranks, -1)
    picks = ranks[:, None, :] == jnp.arange(capacity, dtype=jnp.int32)[None, :, None]
    row_gate = jnp.sum(jnp.where(picks, gates[:, None, :], 0.0), axis=2)
    picks = picks.astype(jnp.bfloat16).reshape(peers * capacity, count)
    buf = jnp.dot(picks, rows, preferred_element_type=jnp.float32)
    is_grad = jnp.arange(rows.shape[1]) >= width
    scale = jnp.where(is_grad[None, :], row_gate.reshape(-1)[:, None], 1.0)
    return (buf * scale).astype(jnp.bfloat16).reshape(peers, capacity, -1)


def body(
    tokens, grad_out, expert_ids, gate_probs, owner, partner, weight, first_moment, second_moment
):
    peers = lax.axis_size("expert")
    my_index = lax.axis_index("expert")
    swap_bit = peers.bit_length() - 2
    top_k = expert_ids.shape[1]
    expert_count = owner.shape[0]
    capacity = tokens.shape[0] * top_k * 9 // (8 * expert_count)
    width_hidden = weight.shape[2] // 2
    width = tokens.shape[1]
    labels = jnp.arange(expert_count, dtype=jnp.int32)
    moved = jnp.sum(jnp.where(labels == my_index, partner, 0)) != my_index
    slots = jnp.sum(jnp.where(expert_ids[:, :, None] == labels, owner, 0), axis=2)
    half = peers // 2
    upper = my_index >= half
    gates = plane_gates(slots, gate_probs, peers)
    low_gates, high_gates = gates[:half], gates[half:]
    packed = jnp.concatenate([tokens, grad_out], axis=1)
    other_rows = from_partner(packed, "expert", swap_bit)
    other_gates = from_partner(jnp.where(upper, low_gates, high_gates), "expert", swap_bit)
    other_rows, weight = lax.optimization_barrier((other_rows, weight))
    buf = routed_rows(
        jnp.concatenate([packed, other_rows], axis=0),
        jnp.concatenate([jnp.where(upper, high_gates, low_gates), other_gates], axis=1),
        width,
        2 * capacity,
    )
    planes = [list(range(half)), list(range(half, peers))]
    recv = lax.all_to_all(
        buf, "expert", split_axis=0, concat_axis=0, tiled=True, axis_index_groups=planes
    ).reshape(half * 2 * capacity, -1)
    rows_in = recv[:, :width]
    rows_grad = recv[:, width:]
    pre_act = jnp.dot(
        rows_in,
        lax.all_gather(weight, "dp", axis=1, tiled=True)[0],
        preferred_element_type=jnp.float32,
    )
    back = rows_grad.astype(jnp.float32)
    gate_part = pre_act[:, :width_hidden]
    up_part = pre_act[:, width_hidden:]
    sigma = jax.nn.sigmoid(gate_part)
    silu_value = gate_part * sigma
    slope = sigma * (1.0 + gate_part * (1.0 - sigma))
    contract = (((0,), (0,)), ((), ()))
    first_old = first_moment[0].astype(jnp.float32)
    second_old = second_moment[0].astype(jnp.float32)
    deltas = lax.optimization_barrier(
        ((back * up_part * slope).astype(jnp.bfloat16), (back * silu_value).astype(jnp.bfloat16))
    )
    partials = [
        lax.dot_general(rows_in, delta, contract, preferred_element_type=jnp.float32).astype(
            jnp.bfloat16
        )
        for delta in deltas
    ]
    outputs = []
    arrived = None
    for part in range(2):
        columns = slice(part * width_hidden, (part + 1) * width_hidden)
        grads = lax.psum_scatter(partials[part], "dp", scatter_dimension=0, tiled=True)
        if part == 1:
            grads, arrived = lax.optimization_barrier((grads, arrived))
            outputs.append(jnp.where(moved, arrived.astype(jnp.float32), step))
        grads = grads.astype(jnp.float32)
        first_new = BETA_ONE * first_old[:, columns] + (1.0 - BETA_ONE) * grads
        second_new = BETA_TWO * second_old[:, columns] + (1.0 - BETA_TWO) * grads * grads
        step = first_new / (jnp.sqrt(second_new) + EPSILON)
        sent = step.astype(jnp.bfloat16)
        if part == 0:
            sent, partials[1] = lax.optimization_barrier((sent, partials[1]))
        arrived = from_partner(sent, "expert", swap_bit)
    outputs.append(jnp.where(moved, arrived.astype(jnp.float32), step))
    return jnp.concatenate(outputs, axis=1)[None]


def solution(mesh):
    in_specs = (
        P(("dp", "expert"), None),
        P(("dp", "expert"), None),
        P(("dp", "expert"), None),
        P(("dp", "expert"), None),
        P(),
        P(),
        P("expert", "dp", None),
        P("expert", "dp", None),
        P("expert", "dp", None),
    )
    out_specs = P("expert", "dp", None)
    return jax.shard_map(body, mesh=mesh, in_specs=in_specs, out_specs=out_specs, check_vma=False)
```

```python
import jax
import jax.numpy as jnp
from jax import lax
from jax.sharding import PartitionSpec as P

BETA_ONE = 0.9
BETA_TWO = 0.95
EPSILON = 1e-08


def from_partner(value, axis, bit):
    mask = 2**bit
    pairs = [(source, source ^ mask) for source in range(lax.axis_size(axis))]
    return lax.ppermute(value, axis, pairs)


def plane_gates(slots, gate_probs, peers):
    labels = jnp.arange(peers, dtype=jnp.int32)
    hit = slots[None, :, :] == labels[:, None, None]
    return jnp.sum(jnp.where(hit, gate_probs[None], 0.0), axis=2)


def routed_rows(rows, gates, width, capacity):
    peers, count = gates.shape
    chosen = gates > 0.0
    before = jnp.arange(count)[:, None] < jnp.arange(count)[None, :]
    ranks = jnp.dot(
        chosen.astype(jnp.bfloat16), before.astype(jnp.bfloat16), preferred_element_type=jnp.float32
    ).astype(jnp.int32)
    ranks = jnp.where(chosen, ranks, -1)
    picks = ranks[:, None, :] == jnp.arange(capacity, dtype=jnp.int32)[None, :, None]
    row_gate = jnp.sum(jnp.where(picks, gates[:, None, :], 0.0), axis=2)
    picks = picks.astype(jnp.bfloat16).reshape(peers * capacity, count)
    buf = jnp.dot(picks, rows, preferred_element_type=jnp.float32)
    is_grad = jnp.arange(rows.shape[1]) >= width
    scale = jnp.where(is_grad[None, :], row_gate.reshape(-1)[:, None], 1.0)
    return (buf * scale).astype(jnp.bfloat16).reshape(peers, capacity, -1)


def ring_sum(rows_in, delta, way):
    devices = lax.axis_size("dp")
    chips = devices // 2
    height = rows_in.shape[1] // devices
    index = lax.axis_index("dp")
    chip, core = index // 2, index % 2
    swap = [(source, source ^ 1) for source in range(devices)]
    onward = [(source, (source + 2 * way) % devices) for source in range(devices)]

    def product(owner):
        rows = lax.dynamic_slice_in_dim(rows_in, owner * height, height, axis=1)
        contract = (((0,), (0,)), ((), ()))
        return lax.dot_general(rows, delta, contract, preferred_element_type=jnp.float32)

    total = None
    for hop in range(chips):
        target = (chip - way * (hop + 1)) % chips
        theirs = product(2 * target + 1 - core).astype(jnp.bfloat16)
        term = product(2 * target + core) + lax.ppermute(theirs, "dp", swap).astype(jnp.float32)
        if total is not None:
            term += lax.ppermute(total, "dp", onward).astype(jnp.float32)
        total = term.astype(jnp.bfloat16)
    return term


def body(
    tokens, grad_out, expert_ids, gate_probs, owner, partner, weight, first_moment, second_moment
):
    peers = lax.axis_size("expert")
    my_index = lax.axis_index("expert")
    swap_bit = peers.bit_length() - 2
    top_k = expert_ids.shape[1]
    expert_count = owner.shape[0]
    capacity = tokens.shape[0] * top_k * 9 // (8 * expert_count)
    width_hidden = weight.shape[2] // 2
    width = tokens.shape[1]
    labels = jnp.arange(expert_count, dtype=jnp.int32)
    moved = jnp.sum(jnp.where(labels == my_index, partner, 0)) != my_index
    slots = jnp.sum(jnp.where(expert_ids[:, :, None] == labels, owner, 0), axis=2)
    half = peers // 2
    upper = my_index >= half
    gates = plane_gates(slots, gate_probs, peers)
    low_gates, high_gates = gates[:half], gates[half:]
    packed = jnp.concatenate([tokens, grad_out], axis=1)
    other_rows = from_partner(packed, "expert", swap_bit)
    other_gates = from_partner(jnp.where(upper, low_gates, high_gates), "expert", swap_bit)
    other_rows, weight = lax.optimization_barrier((other_rows, weight))
    buf = routed_rows(
        jnp.concatenate([packed, other_rows], axis=0),
        jnp.concatenate([jnp.where(upper, high_gates, low_gates), other_gates], axis=1),
        width,
        2 * capacity,
    )
    planes = [list(range(half)), list(range(half, peers))]
    recv = lax.all_to_all(
        buf, "expert", split_axis=0, concat_axis=0, tiled=True, axis_index_groups=planes
    ).reshape(half * 2 * capacity, -1)
    rows_in = recv[:, :width]
    rows_grad = recv[:, width:]
    pre_act = jnp.dot(
        rows_in,
        lax.all_gather(weight, "dp", axis=1, tiled=True)[0],
        preferred_element_type=jnp.float32,
    )
    back = rows_grad.astype(jnp.float32)
    gate_part = pre_act[:, :width_hidden]
    up_part = pre_act[:, width_hidden:]
    sigma = jax.nn.sigmoid(gate_part)
    silu_value = gate_part * sigma
    slope = sigma * (1.0 + gate_part * (1.0 - sigma))
    deltas = lax.optimization_barrier(
        ((back * up_part * slope).astype(jnp.bfloat16), (back * silu_value).astype(jnp.bfloat16))
    )
    grads = jnp.concatenate(
        [ring_sum(rows_in, deltas[0], 1), ring_sum(rows_in, deltas[1], -1)], axis=1
    )
    first_new = BETA_ONE * first_moment[0].astype(jnp.float32) + (1.0 - BETA_ONE) * grads
    second_new = BETA_TWO * second_moment[0].astype(jnp.float32) + (1.0 - BETA_TWO) * grads * grads
    step = first_new / (jnp.sqrt(second_new) + EPSILON)
    arrived = from_partner(step.astype(jnp.bfloat16), "expert", swap_bit)
    return jnp.where(moved, arrived.astype(jnp.float32), step)[None]


def solution(mesh):
    in_specs = (
        P(("dp", "expert"), None),
        P(("dp", "expert"), None),
        P(("dp", "expert"), None),
        P(("dp", "expert"), None),
        P(),
        P(),
        P("expert", "dp", None),
        P("expert", "dp", None),
        P("expert", "dp", None),
    )
    out_specs = P("expert", "dp", None)
    return jax.shard_map(body, mesh=mesh, in_specs=in_specs, out_specs=out_specs, check_vma=False)
```
